128 devices in a mesh: rep: 8 (over y, core), sp: 16 (over z, x).
Axes of the slice: x: 4, y: 4, z: 4, core: 2. Of those that a mesh axis runs over, the one named last changes fastest.
Arguments:
- queries: bfloat16 [32768, 8192], P(('rep', 'sp')), may hold values from -12 to 12
- keys: bfloat16 [32768, 1024], P(('rep', 'sp')), may hold values from -12 to 12
- values: bfloat16 [32768, 1024], P(('rep', 'sp')), may hold values from -6 to 6
- doc_lengths: int32 [8, 16], P('rep'), may hold values from 1 to 1024, 4096 in all within a row
- dest_group: int32 [8, 128], replicated, may hold values from 0 to 7, as said below
- dest_slot: int32 [8, 128], replicated, may hold values from 0 to 7, as said below
Outputs:
- attended: bfloat16 [32768, 8192], P(('rep', 'sp'))
The draws below stay inside these ranges and needn't reach their ends.
Inputs may be any that keep to these rules, and one draw needn't show every extreme that they name: Piece j of sp index s of group g goes to the same sp index of group dest_group[g, s * 8 + j]; the 8 pieces of each device go to exactly half of the 8 groups, 2 to each. `dest_slot`: on every device of every group each of the 8 slots receives exactly one piece.
All inputs are finite; a program needn't handle non-finite values.
Results may differ from the reference program's by a relative error of at most 0.004.
Values may be sent and summed in bfloat16 or wider, within the bound.
No kernel may reach another device: no remote copies, remote signals or barrier semaphores. Data moves between devices by JAX's collectives and lax.ppermute only.
A program may use at most 192 MiB of HBM per device.

```python
import math
import jax
import jax.numpy as jnp
import numpy as np
from jax import lax

QUERY_HEADS = 64
KEY_VALUE_HEADS = 8
HEAD_WIDTH = 128
DEVICE_PIECES = 8
TILE_ROWS = 512
NDOC = 16
PIECE_LENGTH = 32
STREAM = 4096
TOKEN_TOTAL = 32768
MOSTDOC = 1024
N_REP = 8
N_SP = 16


def route_tables(key):
    folded = jax.random.fold_in(key, 71)
    key_sigma, key_source, key_target = jax.random.split(folded, 3)
    capacity = 2 * DEVICE_PIECES // N_REP
    sigma = jax.vmap(lambda inner: jax.random.permutation(inner, N_REP))(jax.random.split(key_sigma, N_SP))
    source_perm = jax.vmap(lambda inner: jax.random.permutation(inner, DEVICE_PIECES))(jax.random.split(key_source, N_REP * N_SP)).reshape(N_REP, N_SP, DEVICE_PIECES)
    target_perm = jax.vmap(lambda inner: jax.random.permutation(inner, DEVICE_PIECES))(jax.random.split(key_target, N_REP * N_SP)).reshape(N_REP, N_SP, DEVICE_PIECES)
    groups = jnp.arange(N_REP, dtype=jnp.int32)[:, None, None]
    shards = jnp.arange(N_SP, dtype=jnp.int32)[None, :, None]
    orders = jnp.arange(DEVICE_PIECES, dtype=jnp.int32)[None, None, :]
    target = sigma[shards, (groups + orders // capacity) % N_REP]
    slot_table = target_perm[target, shards, orders]
    inverse = jnp.argsort(source_perm, axis=2)
    group_out = jnp.take_along_axis(target, inverse, axis=2)
    slot_out = jnp.take_along_axis(slot_table, inverse, axis=2)
    return (group_out.reshape(N_REP, N_SP * DEVICE_PIECES).astype(jnp.int32), slot_out.reshape(N_REP, N_SP * DEVICE_PIECES).astype(jnp.int32))


def draw_dest_group(key, part):
    return route_tables(key)[0]


def draw_dest_slot(key, part):
    return route_tables(key)[1]


def query_key(key):
    folded = jax.random.fold_in(key, 29)
    key_query, random_key_seed = jax.random.split(folded, 2)
    query_row_data = jax.random.truncated_normal(key_query, -6.0, 6.0, (TOKEN_TOTAL, QUERY_HEADS * HEAD_WIDTH), jnp.float32)
    key_row_data = jax.random.truncated_normal(random_key_seed, -6.0, 6.0, (TOKEN_TOTAL, KEY_VALUE_HEADS * HEAD_WIDTH), jnp.float32)
    return (query_row_data, key_row_data)


def draw_queries(key, part):
    return query_key(key)[0].astype(jnp.bfloat16)


def draw_keys(key, part):
    return query_key(key)[1].astype(jnp.bfloat16)


def shard_levels(key, dims, cuts, smallest, largest):
    loudness, own = 1.0, jax.random.fold_in(key, 6)
    for axis_at, shards_of in cuts:
        draws = jnp.exp(jax.random.uniform(jax.random.fold_in(own, axis_at), (shards_of,), jnp.float32, smallest / len(cuts), largest / len(cuts)))
        loudness = loudness * jnp.repeat(draws, dims[axis_at] // shards_of).reshape([-1 if axis == axis_at else 1 for axis in range(len(dims))])
    return loudness


def profile(count, total, reach, skew):
    weights = [(1 << 20) // math.isqrt(standing ** skew) + 1 for standing in range(2, count + 1)]
    rest, given = total - reach - (count - 1), [1] * (count - 1)
    while rest > 0:
        candidates = [i for i in range(count - 1) if given[i] < reach]
        whole, left = sum([weights[i] for i in candidates]), rest
        for i in candidates:
            extra = min(reach - given[i], max(1, left * weights[i] // whole), rest)
            given[i] = given[i] + extra
            rest = rest - extra
    return np.array([reach] + given)


def ragged_sizes(key, count, total, bound, skew):
    if count == 2:
        one = jax.random.randint(key, (), max(1, total - bound), min(bound, total - 1) + 1)
        return jnp.stack([one, total - one])
    sizes = jnp.asarray(profile(count, total, bound, skew), jnp.int32)
    couples = (count - 1) // 2
    source_of, taker = sizes[1:1 + 2 * couples:2], sizes[2:2 + 2 * couples:2]
    slack = jnp.minimum(source_of - 1, bound - taker)
    passed = jax.random.randint(jax.random.fold_in(key, 1), (couples,), 0, 1 << 20) % (slack + 1)
    sizes = sizes.at[1:1 + 2 * couples:2].set(source_of - passed).at[2:2 + 2 * couples:2].set(taker + passed)
    return sizes[jax.random.permutation(jax.random.fold_in(key, 2), count)]


def bell_draw(key, dims, scale, most, cuts=(), kind=jnp.bfloat16):
    level = shard_levels(key, dims, cuts, -0.22, 0.18) if cuts else 1.0
    entries = jax.random.normal(key, dims, jnp.float32) * scale * level
    return jnp.minimum(jnp.maximum(entries, -most), most).astype(kind)


def setup_inputs(seed: int = 0) -> dict:
    arg_keys = jax.random.split(jax.random.key(seed), 7)
    return {
        "queries": draw_queries(jax.random.fold_in(arg_keys[6], 71), 0),
        "keys": draw_keys(jax.random.fold_in(arg_keys[6], 71), 0),
        "values": bell_draw(arg_keys[2], (TOKEN_TOTAL, KEY_VALUE_HEADS * HEAD_WIDTH), 1.0, 6.0, ((0, 128),)),
        "doc_lengths": jax.vmap(lambda own: ragged_sizes(own, NDOC, STREAM, MOSTDOC, 2))(jax.random.split(arg_keys[3], N_REP)).reshape((N_REP, NDOC)).astype(jnp.int32),
        "dest_group": draw_dest_group(jax.random.fold_in(arg_keys[6], 71), 0),
        "dest_slot": draw_dest_slot(jax.random.fold_in(arg_keys[6], 71), 0),
    }


MASKED = -1e+30

def doc_starts(positions, lengths):
    doc_ends = jnp.cumsum(lengths)
    return lax.optimization_barrier(jnp.sum(jnp.where(positions[:, None] >= doc_ends[None, :], lengths[None, :], 0), axis=1))

def place_pieces(row_data, dest_group, dest_slot):
    feature_width = row_data.shape[1]
    pieces = row_data.reshape(N_REP * N_SP * DEVICE_PIECES, PIECE_LENGTH, feature_width)
    shard_index = (jnp.arange(N_SP * DEVICE_PIECES, dtype=jnp.int32) // DEVICE_PIECES)[None, :]
    target = (dest_group * (N_SP * DEVICE_PIECES) + shard_index * DEVICE_PIECES + dest_slot).reshape(-1).astype(jnp.int32)
    placed = jnp.zeros_like(pieces).at[target].set(pieces)
    return placed.reshape(N_REP, STREAM, feature_width)

def group_attention(operands):
    grouped_queries, grouped_keys, grouped_values, lengths = operands
    positions = jnp.arange(STREAM, dtype=jnp.int32)
    starts = doc_starts(positions, lengths)
    heads_per_group = QUERY_HEADS // KEY_VALUE_HEADS
    score_scale = 1.0 / math.sqrt(HEAD_WIDTH)
    blocks = []
    for block_index in range(STREAM // TILE_ROWS):
        row_begin = block_index * TILE_ROWS
        row_stop = row_begin + TILE_ROWS
        allowed = (starts[row_begin:row_stop, None] == starts[None, :row_stop]) & (positions[row_begin:row_stop, None] >= positions[None, :row_stop])

        def one_head(head_ops, allowed=allowed):
            head_query, head_key, head_value = head_ops
            scores = jnp.einsum('qgd,kd->qgk', head_query.astype(jnp.float32), head_key.astype(jnp.float32)) * score_scale
            scores = jnp.where(allowed[:, None, :], scores, MASKED)
            row_peak = lax.optimization_barrier(jnp.max(scores, axis=2, keepdims=True))
            exponent = jnp.exp(scores - row_peak)
            row_total = lax.optimization_barrier(jnp.sum(exponent, axis=2))
            weights = exponent.astype(jnp.bfloat16)
            summed = jnp.einsum('qgk,kd->qgd', weights.astype(jnp.float32), head_value.astype(jnp.float32))
            return summed / row_total[:, :, None]
        query_block_rows = grouped_queries[row_begin:row_stop].reshape(TILE_ROWS, KEY_VALUE_HEADS, heads_per_group, HEAD_WIDTH).transpose(1, 0, 2, 3)
        key_block_rows = grouped_keys[:row_stop].reshape(row_stop, KEY_VALUE_HEADS, HEAD_WIDTH).transpose(1, 0, 2)
        value_block_rows = grouped_values[:row_stop].reshape(row_stop, KEY_VALUE_HEADS, HEAD_WIDTH).transpose(1, 0, 2)
        result = lax.map(one_head, (query_block_rows, key_block_rows, value_block_rows))
        blocks.append(result.transpose(1, 0, 2, 3).reshape(TILE_ROWS, QUERY_HEADS * HEAD_WIDTH))
    return jnp.concatenate(blocks, axis=0)

def reference(queries, keys, values, doc_lengths, dest_group, dest_slot):
    placed_query = place_pieces(queries, dest_group, dest_slot)
    placed_key = place_pieces(keys, dest_group, dest_slot)
    placed_value = place_pieces(values, dest_group, dest_slot)
    outputs = lax.map(group_attention, (placed_query, placed_key, placed_value, doc_lengths))
    return outputs.reshape(TOKEN_TOTAL, QUERY_HEADS * HEAD_WIDTH).astype(jnp.bfloat16)
```

```python
import functools
import math

import jax
import jax.numpy as jnp
from jax import lax
from jax.experimental import pallas as pl
from jax.experimental.pallas import tpu as pltpu
from jax.sharding import PartitionSpec as P

QUERY_HEADS = 64
KEY_VALUE_HEADS = 8
HEADS_PER_KEY = QUERY_HEADS // KEY_VALUE_HEADS
HEAD_WIDTH = 128
PIECES = 8
PIECE = 32
GROUPS = 8
CAPACITY = 2
NDOC = 16
BLOCK = PIECES * PIECE
BACK = 4
LINE = 4
KEY_TILE = 128
MOST_TILES = 9
QUERY_WIDTH = QUERY_HEADS * HEAD_WIDTH
KEY_WIDTH = KEY_VALUE_HEADS * HEAD_WIDTH
MASKED = -1e30
EXPONENT_SCALE = 1.0 / math.sqrt(HEAD_WIDTH) / math.log(2.0)

ANY = pl.BlockSpec(memory_space=pl.ANY)
SMEM = pl.BlockSpec(memory_space=pltpu.SMEM)


def pack_kernel(source_count, meta, groups, *refs):
    sources = refs[:source_count]
    outs = refs[source_count : source_count + GROUPS]
    held, in_sems, out_sems = refs[-3:]
    group_self, shard = meta[0], meta[1]
    targets = [groups[group_self, shard * PIECES + j] for j in range(PIECES)]

    def copies_in(j):
        column = 0
        made = []
        for k, source in enumerate(sources):
            width = source.shape[1]
            made.append(
                pltpu.make_async_copy(
                    source.at[pl.ds(j * PIECE, PIECE)],
                    held.at[j, :, pl.ds(column, width)],
                    in_sems.at[k, j],
                )
            )
            column += width
        return made

    def copy_out(j, rotation, place):
        return pltpu.make_async_copy(
            held.at[j], outs[rotation].at[pl.ds(place * PIECE, PIECE)], out_sems.at[j]
        )

    for j in range(PIECES):
        for copy in copies_in(j):
            copy.start()

    for j in range(PIECES):
        place = jnp.int32(0)
        for earlier in range(j):
            place += (targets[earlier] == targets[j]).astype(jnp.int32)
        rotation_of = lax.rem(targets[j] - group_self + GROUPS, GROUPS)
        for copy in copies_in(j):
            copy.wait()
        for rotation in range(GROUPS):

            @pl.when(rotation_of == rotation)
            def _():
                copy_out(j, rotation, place).start()

    for j in range(PIECES):
        copy_out(j, 0, 0).wait()


def pack(meta, groups, *sources):
    width = sum(source.shape[1] for source in sources)
    return pl.pallas_call(
        functools.partial(pack_kernel, len(sources)),
        out_shape=[
            jax.ShapeDtypeStruct((CAPACITY * PIECE, width), jnp.bfloat16) for _ in range(GROUPS)
        ],
        in_specs=[SMEM, SMEM] + [ANY] * len(sources),
        out_specs=[ANY] * GROUPS,
        scratch_shapes=[
            pltpu.VMEM((PIECES, PIECE, width), jnp.bfloat16),
            pltpu.SemaphoreType.DMA((len(sources), PIECES)),
            pltpu.SemaphoreType.DMA((PIECES,)),
        ],
        compiler_params=pltpu.CompilerParams(vmem_limit_bytes=12 << 20),
        name="pack",
    )(meta, groups, *sources)


def arrivals(meta, groups, slots, rotation):
    group_self, shard = meta[0], meta[1]
    source = lax.rem(group_self - rotation + GROUPS, GROUPS)
    found = []
    place = jnp.int32(0)
    for j in range(PIECES):
        here = groups[source, shard * PIECES + j] == group_self
        found.append((here, place, slots[source, shard * PIECES + j]))
        place += here.astype(jnp.int32)
    return found


def place_kernel(meta, groups, slots, *refs):
    arrived, out = refs[:GROUPS], refs[GROUPS]
    held, in_sems, out_sem = refs[-3:]

    def copy_of(rotation, place, slot):
        return pltpu.make_async_copy(
            arrived[rotation].at[pl.ds(place * PIECE, PIECE)],
            held.at[pl.ds(slot * PIECE, PIECE)],
            in_sems.at[slot],
        )

    for rotation in range(GROUPS):
        for here, place, slot in arrivals(meta, groups, slots, rotation):

            @pl.when(here)
            def _():
                copy_of(rotation, place, slot).start()

    for slot in range(PIECES):
        copy_of(0, 0, slot).wait()
    whole = pltpu.make_async_copy(held, out, out_sem)
    whole.start()
    whole.wait()


def place_keys(meta, groups, slots, arrived):
    return pl.pallas_call(
        place_kernel,
        out_shape=jax.ShapeDtypeStruct((BLOCK, arrived[0].shape[1]), jnp.bfloat16),
        in_specs=[SMEM] * 3 + [ANY] * GROUPS,
        out_specs=ANY,
        scratch_shapes=[
            pltpu.VMEM((BLOCK, arrived[0].shape[1]), jnp.bfloat16),
            pltpu.SemaphoreType.DMA((PIECES,)),
            pltpu.SemaphoreType.DMA,
        ],
        compiler_params=pltpu.CompilerParams(vmem_limit_bytes=4 << 20),
        name="place_keys",
    )(meta, groups, slots, *arrived)


def piece_attention(tiles, row, first_tile, query_ref, window, bias, out_ref, out_slot):
    span = tiles * KEY_TILE
    begin = pl.multiple_of(first_tile * KEY_TILE, KEY_TILE)

    def one_head(head, _):
        at = pl.multiple_of(head * HEAD_WIDTH, HEAD_WIDTH)
        query_at = head * (HEADS_PER_KEY * HEAD_WIDTH)
        query = jnp.concatenate(
            [
                query_ref[
                    pl.ds(row, PIECE),
                    pl.ds(pl.multiple_of(query_at + k * HEAD_WIDTH, HEAD_WIDTH), HEAD_WIDTH),
                ]
                for k in range(HEADS_PER_KEY)
            ],
            axis=0,
        )
        key = window[pl.ds(begin, span), pl.ds(at, HEAD_WIDTH)]
        value = window[
            pl.ds(begin, span), pl.ds(pl.multiple_of(KEY_WIDTH + at, HEAD_WIDTH), HEAD_WIDTH)
        ]
        scores = lax.dot_general(
            query, key, (((1,), (1,)), ((), ())), preferred_element_type=jnp.float32
        )
        scores = (
            scores.reshape(HEADS_PER_KEY, PIECE, span) + bias[:, pl.ds(0, span)][None]
        ).reshape(HEADS_PER_KEY * PIECE, span)
        peak = jnp.max(scores, axis=1, keepdims=True)
        weights = jnp.exp2((scores - peak) * EXPONENT_SCALE)
        total = jnp.sum(weights, axis=1, keepdims=True)
        summed = jnp.dot(
            weights.astype(jnp.bfloat16), value, preferred_element_type=jnp.float32
        )
        result = (summed * (1.0 / total)).astype(jnp.bfloat16)
        for k in range(HEADS_PER_KEY):
            out_ref[
                out_slot,
                :,
                pl.ds(pl.multiple_of(query_at + k * HEAD_WIDTH, HEAD_WIDTH), HEAD_WIDTH),
            ] = result[k * PIECE : (k + 1) * PIECE]
        return 0

    lax.fori_loop(0, KEY_VALUE_HEADS, one_head, 0, unroll=2)


def attend_kernel(rotations, first, meta, groups, slots, lengths, *refs):
    count = len(rotations)
    arrived = refs[:count]
    own, left1, left2, left3, back4, back3, back2, back1 = refs[count : count + 8]
    out = refs[count + 8 + (0 if first else 1)]
    listed, query, window, bias, result, query_sems, window_sems, out_sems = refs[-8:]
    shard = meta[1]
    line_at = lax.rem(shard, LINE)

    total = jnp.int32(0)
    for i, rotation in enumerate(rotations):
        for here, place, slot in arrivals(meta, groups, slots, rotation):

            @pl.when(here)
            def _():
                listed[0, total] = (i * CAPACITY + place) * PIECE
                listed[1, total] = slot

            total = total + here.astype(jnp.int32)

    def query_copy(i):
        rows = CAPACITY * PIECE
        return pltpu.make_async_copy(
            arrived[i], query.at[pl.ds(i * rows, rows)], query_sems.at[i]
        )

    def window_copy(source, block):
        return pltpu.make_async_copy(
            source, window.at[pl.ds(block * BLOCK, BLOCK)], window_sems.at[block]
        )

    @pl.when(total > 0)
    def _():
        for i in range(count):
            query_copy(i).start()
        window_copy(own, BACK).start()
        window_copy(back4, 0).start()
        for block, least, near, far in ((3, 1, left1, back1), (2, 2, left2, back2), (1, 3, left3, back3)):

            @pl.when(line_at >= least)
            def _():
                window_copy(near, block).start()

            @pl.when(line_at < least)
            def _():
                window_copy(far, block).start()

        for i in range(count):
            query_copy(i).wait()
        for block in range(BACK + 1):
            window_copy(own, block).wait()

        def out_copy(index, slot):
            at = lax.rem(index, 2)
            return pltpu.make_async_copy(
                result.at[at], out.at[pl.ds(slot * PIECE, PIECE)], out_sems.at[at]
            )

        def one_piece(index, _):
            row = pl.multiple_of(listed[0, index], PIECE)
            slot = listed[1, index]
            base = (shard - BACK) * BLOCK
            begin = shard * BLOCK + slot * PIECE
            place = begin + lax.broadcasted_iota(jnp.int32, (PIECE, KEY_TILE), 0)
            start = jnp.zeros((PIECE, KEY_TILE), jnp.int32)
            first_start = jnp.int32(0)
            end = jnp.int32(0)
            for d in range(NDOC):
                end = end + lengths[0, d]
                start = jnp.where(place >= end, end, start)
                first_start = jnp.where(begin >= end, end, first_start)
            first_tile = (first_start - base) // KEY_TILE
            tiles = (begin - base + PIECE - 1) // KEY_TILE - first_tile + 1
            lane = lax.broadcasted_iota(jnp.int32, (PIECE, KEY_TILE), 1)

            def one_bias(k, _):
                at = lane + (base + (first_tile + k) * KEY_TILE)
                bias[:, pl.ds(pl.multiple_of(k * KEY_TILE, KEY_TILE), KEY_TILE)] = jnp.where(
                    (at >= start) & (at <= place), 0.0, MASKED
                )
                return 0

            lax.fori_loop(0, tiles, one_bias, 0)

            @pl.when(index >= 2)
            def _():
                out_copy(index, 0).wait()

            for known in range(1, MOST_TILES + 1):

                @pl.when(tiles == known)
                def _():
                    piece_attention(
                        known, row, first_tile, query, window, bias, result, lax.rem(index, 2)
                    )

            out_copy(index, slot).start()
            return 0

        lax.fori_loop(0, total, one_piece, 0)

        @pl.when(total >= 2)
        def _():
            out_copy(total, 0).wait()

        out_copy(total + 1, 0).wait()


def attend(rotations, meta, groups, slots, lengths, arrived, blocks, out):
    first = out is None
    count = len(rotations)
    operands = [meta, groups, slots, lengths, *arrived, *blocks] + ([] if first else [out])
    return pl.pallas_call(
        functools.partial(attend_kernel, rotations, first),
        out_shape=jax.ShapeDtypeStruct((BLOCK, QUERY_WIDTH), jnp.bfloat16),
        in_specs=[SMEM] * 4 + [ANY] * (len(operands) - 4),
        out_specs=ANY,
        scratch_shapes=[
            pltpu.SMEM((2, count * CAPACITY), jnp.int32),
            pltpu.VMEM((count * CAPACITY * PIECE, QUERY_WIDTH), jnp.bfloat16),
            pltpu.VMEM(((BACK + 1) * BLOCK, 2 * KEY_WIDTH), jnp.bfloat16),
            pltpu.VMEM((PIECE, MOST_TILES * KEY_TILE), jnp.float32),
            pltpu.VMEM((2, PIECE, QUERY_WIDTH), jnp.bfloat16),
            pltpu.SemaphoreType.DMA((count,)),
            pltpu.SemaphoreType.DMA((BACK + 1,)),
            pltpu.SemaphoreType.DMA((2,)),
        ],
        input_output_aliases={} if first else {len(operands) - 1: 0},
        compiler_params=pltpu.CompilerParams(vmem_limit_bytes=40 << 20),
        name="attend",
    )(*operands)


def rotate(array, by):
    if by == 0:
        return array
    return lax.ppermute(array, "rep", [(g, (g + by) % GROUPS) for g in range(GROUPS)])


def window_blocks(own, shards):
    def hop(array, pairs):
        return lax.ppermute(array, "sp", pairs)

    def along(froms, step, rows):
        return [(z * LINE + x, z * LINE + (x + step) % LINE) for z in rows for x in froms]

    lines = shards // LINE
    every, later = range(lines), range(1, lines)
    back4 = hop(own, [(s, s + LINE) for s in range(shards - LINE)])
    left1 = hop(own, along((0, 1, 2), 1, every))
    left3 = hop(own, along((0,), -1, every))
    back3 = hop(back4, along((1, 2, 3), -1, later))
    back1 = hop(back4, along((3,), 1, later))
    left2 = hop(left1, along((1, 2), 1, every))
    back2 = hop(back3, along((1, 2), -1, later))
    return own, left1, left2, left3, back4, back3, back2, back1


CHUNKS = ((0, 1, 7, 2, 6), (3, 5), (4,))


def shards(queries, keys, values, doc_lengths, dest_group, dest_slot):
    meta = jnp.stack([lax.axis_index("rep"), lax.axis_index("sp")]).astype(jnp.int32)
    key_packed = pack(meta, dest_group, keys, values)
    key_arrived = [rotate(array, r) for r, array in enumerate(key_packed)]
    query_packed = pack(meta, dest_group, queries)
    query_arrived = [rotate(array, r) for r, array in enumerate(query_packed)]
    own = place_keys(meta, dest_group, dest_slot, key_arrived)
    blocks = window_blocks(own, lax.axis_size("sp"))
    out = None
    for rotations in CHUNKS:
        out = attend(
            rotations,
            meta,
            dest_group,
            dest_slot,
            doc_lengths,
            [query_arrived[r] for r in rotations],
            blocks,
            out,
        )
    return out


def solution(mesh):
    return jax.shard_map(
        shards,
        mesh=mesh,
        in_specs=(
            P(("rep", "sp"), None),
            P(("rep", "sp"), None),
            P(("rep", "sp"), None),
            P("rep", None),
            P(),
            P(),
        ),
        out_specs=P(("rep", "sp"), None),
        check_vma=False,
    )
```

```python
import functools
import math

import jax
import jax.numpy as jnp
from jax import lax
from jax.experimental import pallas as pl
from jax.experimental.pallas import tpu as pltpu
from jax.sharding import PartitionSpec as P

QUERY_HEADS = 64
KEY_VALUE_HEADS = 8
HEADS_PER_KEY = QUERY_HEADS // KEY_VALUE_HEADS
HEAD_WIDTH = 128
PIECES = 8
PIECE = 32
GROUPS = 8
CAPACITY = 2
NDOC = 16
BLOCK = PIECES * PIECE
HALF = BLOCK // 2
BACK = 4
LINE = 4
KEY_TILE = 128
SPANS = (1, 2, 3, 4, 5, 7, 9)
UNROLL = 8
QUERY_WIDTH = QUERY_HEADS * HEAD_WIDTH
KEY_WIDTH = KEY_VALUE_HEADS * HEAD_WIDTH
MASKED = -1e30
EXPONENT_SCALE = 1.0 / math.sqrt(HEAD_WIDTH) / math.log(2.0)

ANY = pl.BlockSpec(memory_space=pl.ANY)
HBM = pl.BlockSpec(memory_space=pltpu.HBM)
SMEM = pl.BlockSpec(memory_space=pltpu.SMEM)


def pack_kernel(source_count, meta, groups, *refs):
    sources = refs[:source_count]
    outs = refs[source_count : source_count + GROUPS]
    held, in_sems, out_sems = refs[-3:]
    group_self, shard = meta[0], meta[1]
    targets = [groups[group_self, shard * PIECES + j] for j in range(PIECES)]

    def copies_in(j):
        column = 0
        made = []
        for k, source in enumerate(sources):
            width = source.shape[1]
            made.append(
                pltpu.make_async_copy(
                    source.at[pl.ds(j * PIECE, PIECE)],
                    held.at[j, :, pl.ds(column, width)],
                    in_sems.at[k, j],
                )
            )
            column += width
        return made

    def copy_out(j, partner, place):
        return pltpu.make_async_copy(
            held.at[j], outs[partner].at[pl.ds(place * PIECE, PIECE)], out_sems.at[j]
        )

    for j in range(PIECES):
        for copy in copies_in(j):
            copy.start()

    for j in range(PIECES):
        place = jnp.int32(0)
        for earlier in range(j):
            place += (targets[earlier] == targets[j]).astype(jnp.int32)
        partner_of = lax.bitwise_xor(targets[j], group_self)
        for copy in copies_in(j):
            copy.wait()
        for partner in range(GROUPS):

            @pl.when(partner_of == partner)
            def _():
                copy_out(j, partner, place).start()

    for j in range(PIECES):
        copy_out(j, 0, 0).wait()


def pack(meta, groups, *sources):
    width = sum(source.shape[1] for source in sources)
    return pl.pallas_call(
        functools.partial(pack_kernel, len(sources)),
        out_shape=[
            jax.ShapeDtypeStruct((CAPACITY * PIECE, width), jnp.bfloat16) for _ in range(GROUPS)
        ],
        in_specs=[SMEM, SMEM] + [HBM] * len(sources),
        out_specs=[HBM] * GROUPS,
        scratch_shapes=[
            pltpu.VMEM((PIECES, PIECE, width), jnp.bfloat16),
            pltpu.SemaphoreType.DMA((len(sources), PIECES)),
            pltpu.SemaphoreType.DMA((PIECES,)),
        ],
        compiler_params=pltpu.CompilerParams(vmem_limit_bytes=12 << 20),
        name="pack",
    )(meta, groups, *sources)


def arrivals(meta, groups, slots, partner):
    group_self, shard = meta[0], meta[1]
    source = lax.bitwise_xor(group_self, partner)
    found = []
    place = jnp.int32(0)
    for j in range(PIECES):
        here = groups[source, shard * PIECES + j] == group_self
        found.append((here, place, slots[source, shard * PIECES + j]))
        place += here.astype(jnp.int32)
    return found


def place_kernel(meta, groups, slots, *refs):
    arrived, out = refs[:GROUPS], refs[GROUPS]
    held, in_sems, out_sem = refs[-3:]

    def copy_of(partner, place, slot):
        return pltpu.make_async_copy(
            arrived[partner].at[pl.ds(place * PIECE, PIECE)],
            held.at[pl.ds(slot * PIECE, PIECE)],
            in_sems.at[slot],
        )

    for partner in range(GROUPS):
        for here, place, slot in arrivals(meta, groups, slots, partner):

            @pl.when(here)
            def _():
                copy_of(partner, place, slot).start()

    for slot in range(PIECES):
        copy_of(0, 0, slot).wait()
    whole = pltpu.make_async_copy(held, out, out_sem)
    whole.start()
    whole.wait()


def place_keys(meta, groups, slots, arrived):
    return pl.pallas_call(
        place_kernel,
        out_shape=jax.ShapeDtypeStruct((BLOCK, arrived[0].shape[1]), jnp.bfloat16),
        in_specs=[SMEM] * 3 + [ANY] * GROUPS,
        out_specs=ANY,
        scratch_shapes=[
            pltpu.VMEM((BLOCK, arrived[0].shape[1]), jnp.bfloat16),
            pltpu.SemaphoreType.DMA((PIECES,)),
            pltpu.SemaphoreType.DMA,
        ],
        compiler_params=pltpu.CompilerParams(vmem_limit_bytes=4 << 20),
        name="place_keys",
    )(meta, groups, slots, *arrived)


def piece_attention(tiles, row, last_tile, query_ref, window, chooser, bias, out_ref, out_slot):
    span = tiles * KEY_TILE
    begin = pl.multiple_of((last_tile + 1 - tiles) * KEY_TILE, KEY_TILE)
    masks = bias[pl.ds(begin, span), :]

    def one_head(head, _):
        at = pl.multiple_of(head * HEAD_WIDTH, HEAD_WIDTH)
        query_at = head * (HEADS_PER_KEY * HEAD_WIDTH)
        query = jnp.concatenate(
            [
                query_ref[
                    pl.ds(row, PIECE),
                    pl.ds(pl.multiple_of(query_at + k * HEAD_WIDTH, HEAD_WIDTH), HEAD_WIDTH),
                ]
                for k in range(HEADS_PER_KEY)
            ],
            axis=0,
        )
        key = window[pl.ds(begin, span), pl.ds(at, HEAD_WIDTH)]
        value = window[
            pl.ds(begin, span), pl.ds(pl.multiple_of(KEY_WIDTH + at, HEAD_WIDTH), HEAD_WIDTH)
        ]
        scores = lax.dot_general(
            jnp.concatenate([query, chooser[...]], axis=1),
            jnp.concatenate([key, masks], axis=1),
            (((1,), (1,)), ((), ())),
            preferred_element_type=jnp.float32,
        )
        peak = jnp.max(scores, axis=1, keepdims=True)
        weights = jnp.exp2((scores - peak) * EXPONENT_SCALE).astype(jnp.bfloat16)
        summed = jnp.dot(
            weights,
            jnp.concatenate([value, jnp.ones_like(value)], axis=1),
            preferred_element_type=jnp.float32,
        )
        result = (summed[:, :HEAD_WIDTH] * (1.0 / summed[:, HEAD_WIDTH:])).astype(jnp.bfloat16)
        for k in range(HEADS_PER_KEY):
            out_ref[
                out_slot,
                :,
                pl.ds(pl.multiple_of(query_at + k * HEAD_WIDTH, HEAD_WIDTH), HEAD_WIDTH),
            ] = result[k * PIECE : (k + 1) * PIECE]
        return 0

    lax.fori_loop(0, KEY_VALUE_HEADS, one_head, 0, unroll=UNROLL)


def attend_kernel(partners, first, meta, groups, slots, lengths, *refs):
    count = len(partners)
    arrived = refs[:count]
    own, left1, left2, far2, right, far3_low, far3_high, back4 = refs[count : count + 8]
    out = refs[count + 8 + (0 if first else 1)]
    listed, query, window, chooser, bias, result, query_sems, window_sems, out_sems = refs[-9:]
    shard = meta[1]
    line_at = lax.rem(shard, LINE)

    total = jnp.int32(0)
    for i, partner in enumerate(partners):
        for here, place, slot in arrivals(meta, groups, slots, partner):

            @pl.when(here)
            def _():
                listed[0, total] = (i * CAPACITY + place) * PIECE
                listed[1, total] = slot

            total = total + here.astype(jnp.int32)

    def query_copy(i):
        rows = CAPACITY * PIECE
        return pltpu.make_async_copy(
            arrived[i], query.at[pl.ds(i * rows, rows)], query_sems.at[i]
        )

    def window_copy(source, block):
        return pltpu.make_async_copy(
            source, window.at[pl.ds(block * BLOCK, BLOCK)], window_sems.at[block]
        )

    def half_copy(source, part):
        return pltpu.make_async_copy(
            source, window.at[pl.ds(BLOCK + part * HALF, HALF)], window_sems.at[1 + part * BACK]
        )

    @pl.when(total > 0)
    def _():
        for i in range(count):
            query_copy(i).start()
        window_copy(own, BACK).start()
        window_copy(back4, 0).start()

        @pl.when(line_at == LINE - 1)
        def _():
            for part in range(2):
                half_copy(right.at[pl.ds(part * HALF, HALF)], part).start()

        @pl.when(line_at < LINE - 1)
        def _():
            half_copy(far3_low, 0).start()
            half_copy(far3_high, 1).start()

        for block, least, near, far in ((3, 1, left1, left2), (2, 2, left2, far2)):

            @pl.when(line_at >= least)
            def _():
                window_copy(near, block).start()

            @pl.when(line_at < least)
            def _():
                window_copy(far, block).start()

        for i in range(count):
            query_copy(i).wait()
        for block in (0, 2, 3, BACK):
            window_copy(own, block).wait()
        for part in range(2):
            half_copy(far3_low, part).wait()

        def out_copy(index, slot):
            at = lax.rem(index, 2)
            return pltpu.make_async_copy(
                result.at[at], out.at[pl.ds(slot * PIECE, PIECE)], out_sems.at[at]
            )

        chosen = lax.broadcasted_iota(jnp.int32, chooser.shape, 0) % PIECE
        lanes = lax.broadcasted_iota(jnp.int32, chooser.shape, 1)
        chooser[...] = jnp.where(chosen == lanes, 1.0, 0.0).astype(jnp.bfloat16)

        def one_piece(index, _):
            row = pl.multiple_of(listed[0, index], PIECE)
            slot = listed[1, index]
            base = (shard - BACK) * BLOCK
            begin = shard * BLOCK + slot * PIECE
            place = begin + lax.broadcasted_iota(jnp.int32, (1, KEY_TILE), 1)
            start = jnp.zeros((1, KEY_TILE), jnp.int32)
            first_start = jnp.int32(0)
            end = jnp.int32(0)
            for d in range(NDOC):
                end = end + lengths[0, d]
                start = jnp.where(place >= end, end, start)
                first_start = jnp.where(begin >= end, end, first_start)
            last_tile = (begin - base + PIECE - 1) // KEY_TILE
            tiles = last_tile - (first_start - base) // KEY_TILE + 1
            span = sum(
                (tiles > least).astype(jnp.int32) * (most - least)
                for least, most in zip((0,) + SPANS[:-1], SPANS)
            )
            first_tile = last_tile + 1 - span
            key_at = base + lax.broadcasted_iota(jnp.int32, (KEY_TILE, KEY_TILE), 0)

            def one_bias(k, _):
                begin_at = pl.multiple_of((first_tile + k) * KEY_TILE, KEY_TILE)
                at = key_at + begin_at
                bias[pl.ds(begin_at, KEY_TILE), :] = jnp.where(
                    (at >= start) & (at <= place), 0.0, MASKED
                ).astype(jnp.bfloat16)
                return 0

            lax.fori_loop(0, span, one_bias, 0)

            @pl.when(index >= 2)
            def _():
                out_copy(index, 0).wait()

            for known in SPANS:

                @pl.when(span == known)
                def _():
                    piece_attention(
                        known,
                        row,
                        last_tile,
                        query,
                        window,
                        chooser,
                        bias,
                        result,
                        lax.rem(index, 2),
                    )

            out_copy(index, slot).start()
            return 0

        lax.fori_loop(0, total, one_piece, 0)

        @pl.when(total >= 2)
        def _():
            out_copy(total, 0).wait()

        out_copy(total + 1, 0).wait()


def attend(partners, meta, groups, slots, lengths, arrived, blocks, out):
    first = out is None
    count = len(partners)
    operands = [meta, groups, slots, lengths, *arrived, *blocks] + ([] if first else [out])
    return pl.pallas_call(
        functools.partial(attend_kernel, partners, first),
        out_shape=jax.ShapeDtypeStruct((BLOCK, QUERY_WIDTH), jnp.bfloat16),
        in_specs=[SMEM] * 4 + [ANY] * (len(operands) - 4),
        out_specs=ANY,
        scratch_shapes=[
            pltpu.SMEM((2, count * CAPACITY), jnp.int32),
            pltpu.VMEM((count * CAPACITY * PIECE, QUERY_WIDTH), jnp.bfloat16),
            pltpu.VMEM(((BACK + 1) * BLOCK, 2 * KEY_WIDTH), jnp.bfloat16),
            pltpu.VMEM((HEADS_PER_KEY * PIECE, KEY_TILE), jnp.bfloat16),
            pltpu.VMEM(((BACK + 1) * BLOCK, KEY_TILE), jnp.bfloat16),
            pltpu.VMEM((2, PIECE, QUERY_WIDTH), jnp.bfloat16),
            pltpu.SemaphoreType.DMA((count,)),
            pltpu.SemaphoreType.DMA((BACK + 2,)),
            pltpu.SemaphoreType.DMA((2,)),
        ],
        input_output_aliases={} if first else {len(operands) - 1: 0},
        compiler_params=pltpu.CompilerParams(vmem_limit_bytes=40 << 20),
        name="attend",
    )(*operands)


def exchange(array, partner):
    if partner == 0:
        return array
    return lax.ppermute(array, "rep", [(g, g ^ partner) for g in range(GROUPS)])


def window_blocks(own, shards):
    line_at = lax.rem(lax.axis_index("sp"), LINE)

    def hop(array, pairs):
        return lax.ppermute(array, "sp", pairs)

    def along(froms, step):
        return [
            (z * LINE + x, z * LINE + (x + step) % LINE)
            for z in range(shards // LINE)
            for x in froms
        ]

    lines = shards // LINE
    half = own.shape[0] // 2
    back4 = hop(own, [(s, s + LINE) for s in range(shards - LINE)])
    right = hop(own, along((0, 1, 2, 3), -1))
    left1 = hop(own, along((0, 1, 2), 1))

    def down(froms, step):
        return [(z * LINE + x, (z + 1) * LINE + x + step) for z in range(lines - 1) for x in froms]

    far2 = hop(right, down((1, 2), -1))
    far3_low = hop(back4[:half], along((1, 2, 3), -1))
    far3_high = hop(right[half:], down((0, 1, 2), 0))
    left2 = hop(jnp.where(line_at == LINE - 1, back4, left1), along((1, 2, 3), 1))
    return own, left1, left2, far2, right, far3_low, far3_high, back4


KEY_ORDER = (2, 6, 3, 7, 4, 5, 1)
QUERY_ORDER = (1, 2, 6, 3, 7, 4, 5)
CHUNKS = ((0, 1, 2, 6), (3, 7), (4, 5))
QUERIES_IN_FLIGHT = 3


def shards(queries, keys, values, doc_lengths, dest_group, dest_slot):
    meta = jnp.stack([lax.axis_index("rep"), lax.axis_index("sp")]).astype(jnp.int32)
    key_packed = pack(meta, dest_group, keys, values)
    query_packed = list(pack(meta, dest_group, queries))
    key_arrived = {0: key_packed[0]}
    query_arrived = {0: query_packed[0]}
    for partner in KEY_ORDER:
        key_arrived[partner] = exchange(key_packed[partner], partner)
    arrived_keys = [key_arrived[partner] for partner in KEY_ORDER]
    for at, partner in enumerate(QUERY_ORDER):
        if at < QUERIES_IN_FLIGHT:
            before = arrived_keys
        else:
            before = query_arrived[QUERY_ORDER[at - QUERIES_IN_FLIGHT]]
        array, _ = lax.optimization_barrier((query_packed[partner], before))
        query_arrived[partner] = exchange(array, partner)
    key_arrived[1], query_packed[0] = lax.optimization_barrier((key_arrived[1], query_packed[0]))
    query_arrived[0] = query_packed[0]
    own = place_keys(meta, dest_group, dest_slot, [key_arrived[r] for r in range(GROUPS)])
    own, query_arrived[1] = lax.optimization_barrier((own, query_arrived[1]))
    blocks = window_blocks(own, lax.axis_size("sp"))
    out = None
    for partners in CHUNKS:
        out = attend(
            partners,
            meta,
            dest_group,
            dest_slot,
            doc_lengths,
            [query_arrived[r] for r in partners],
            blocks,
            out,
        )
    return out


def solution(mesh):
    return jax.shard_map(
        shards,
        mesh=mesh,
        in_specs=(
            P(("rep", "sp"), None),
            P(("rep", "sp"), None),
            P(("rep", "sp"), None),
            P("rep", None),
            P(),
            P(),
        ),
        out_specs=P(("rep", "sp"), None),
        check_vma=False,
    )
```

```python
import functools
import math

import jax
import jax.numpy as jnp
from jax import lax
from jax.experimental import pallas as pl
from jax.experimental.pallas import tpu as pltpu
from jax.sharding import PartitionSpec as P

QUERY_HEADS = 64
KEY_VALUE_HEADS = 8
HEADS_PER_KEY = QUERY_HEADS // KEY_VALUE_HEADS
HEAD_WIDTH = 128
PIECES = 8
PIECE = 32
GROUPS = 8
CAPACITY = 2
NDOC = 16
BLOCK = PIECES * PIECE
HALF = BLOCK // 2
ROWS = HEADS_PER_KEY * PIECE
BACK = 4
LINE = 4
KEY_TILE = 256
MOST_TILES = 5
QUERY_WIDTH = QUERY_HEADS * HEAD_WIDTH
KEY_WIDTH = KEY_VALUE_HEADS * HEAD_WIDTH
MASKED = -1e30
EXPONENT_SCALE = 1.0 / math.sqrt(HEAD_WIDTH) / math.log(2.0)

HBM = pl.BlockSpec(memory_space=pltpu.HBM)
SMEM = pl.BlockSpec(memory_space=pltpu.SMEM)


def pack_kernel(source_count, meta, groups, *refs):
    sources = refs[:source_count]
    outs = refs[source_count : source_count + GROUPS]
    held, in_sems, out_sems = refs[-3:]
    group_self, shard = meta[0], meta[1]
    targets = [groups[group_self, shard * PIECES + j] for j in range(PIECES)]

    def copies_in(j):
        column = 0
        made = []
        for k, source in enumerate(sources):
            width = source.shape[1]
            made.append(
                pltpu.make_async_copy(
                    source.at[pl.ds(j * PIECE, PIECE)],
                    held.at[j, :, pl.ds(column, width)],
                    in_sems.at[k, j],
                )
            )
            column += width
        return made

    def copy_out(j, partner, place):
        return pltpu.make_async_copy(
            held.at[j], outs[partner].at[pl.ds(place * PIECE, PIECE)], out_sems.at[j]
        )

    for j in range(PIECES):
        for copy in copies_in(j):
            copy.start()

    for j in range(PIECES):
        place = jnp.int32(0)
        for earlier in range(j):
            place += (targets[earlier] == targets[j]).astype(jnp.int32)
        partner_of = lax.bitwise_xor(targets[j], group_self)
        for copy in copies_in(j):
            copy.wait()
        for partner in range(GROUPS):

            @pl.when(partner_of == partner)
            def _():
                copy_out(j, partner, place).start()

    for j in range(PIECES):
        copy_out(j, 0, 0).wait()


def pack(meta, groups, *sources):
    width = sum(source.shape[1] for source in sources)
    return pl.pallas_call(
        functools.partial(pack_kernel, len(sources)),
        out_shape=[
            jax.ShapeDtypeStruct((CAPACITY * PIECE, width), jnp.bfloat16) for _ in range(GROUPS)
        ],
        in_specs=[SMEM, SMEM] + [HBM] * len(sources),
        out_specs=[HBM] * GROUPS,
        scratch_shapes=[
            pltpu.VMEM((PIECES, PIECE, width), jnp.bfloat16),
            pltpu.SemaphoreType.DMA((len(sources), PIECES)),
            pltpu.SemaphoreType.DMA((PIECES,)),
        ],
        compiler_params=pltpu.CompilerParams(vmem_limit_bytes=12 << 20),
        name="pack",
    )(meta, groups, *sources)


def arrivals(meta, groups, slots, partner):
    group_self, shard = meta[0], meta[1]
    source = lax.bitwise_xor(group_self, partner)
    found = []
    place = jnp.int32(0)
    for j in range(PIECES):
        here = groups[source, shard * PIECES + j] == group_self
        found.append((here, place, slots[source, shard * PIECES + j]))
        place += here.astype(jnp.int32)
    return found


def place_kernel(meta, groups, slots, *refs):
    arrived, out = refs[:GROUPS], refs[GROUPS]
    held, in_sems, out_sem = refs[-3:]

    def copy_of(partner, place, slot):
        return pltpu.make_async_copy(
            arrived[partner].at[pl.ds(place * PIECE, PIECE)],
            held.at[pl.ds(slot * PIECE, PIECE)],
            in_sems.at[slot],
        )

    for partner in range(GROUPS):
        for here, place, slot in arrivals(meta, groups, slots, partner):

            @pl.when(here)
            def _():
                copy_of(partner, place, slot).start()

    for slot in range(PIECES):
        copy_of(0, 0, slot).wait()
    whole = pltpu.make_async_copy(held, out, out_sem)
    whole.start()
    whole.wait()


def place_keys(meta, groups, slots, arrived):
    return pl.pallas_call(
        place_kernel,
        out_shape=jax.ShapeDtypeStruct((BLOCK, arrived[0].shape[1]), jnp.bfloat16),
        in_specs=[SMEM] * 3 + [HBM] * GROUPS,
        out_specs=HBM,
        scratch_shapes=[
            pltpu.VMEM((BLOCK, arrived[0].shape[1]), jnp.bfloat16),
            pltpu.SemaphoreType.DMA((PIECES,)),
            pltpu.SemaphoreType.DMA,
        ],
        compiler_params=pltpu.CompilerParams(vmem_limit_bytes=4 << 20),
        name="place_keys",
    )(meta, groups, slots, *arrived)


def piece_attention(tiles, row, begin, query_ref, window, bias, scratch, out_ref, out_slot):
    rows, scores, peaks, sums = scratch
    for head in range(KEY_VALUE_HEADS):
        for k in range(HEADS_PER_KEY):
            rows[head, pl.ds(k * PIECE, PIECE), pl.ds(0, HEAD_WIDTH)] = query_ref[
                pl.ds(row, PIECE), pl.ds((head * HEADS_PER_KEY + k) * HEAD_WIDTH, HEAD_WIDTH)
            ]

    def tile_scores(tile, first):
        at = pl.multiple_of(begin + tile * KEY_TILE, HALF)
        masks = bias[pl.ds(at, KEY_TILE), :]
        for head in range(KEY_VALUE_HEADS):
            key = window[pl.ds(at, KEY_TILE), pl.ds(head * HEAD_WIDTH, HEAD_WIDTH)]
            score = lax.dot_general(
                rows[head],
                jnp.concatenate([key, masks], axis=1),
                (((1,), (1,)), ((), ())),
                preferred_element_type=jnp.float32,
            )
            scores[head, tile] = score
            peak = jnp.maximum(score[:, :HEAD_WIDTH], score[:, HEAD_WIDTH:])
            peaks[head] = peak if first else jnp.maximum(peaks[head], peak)

    def tile_sums(tile, first):
        at = pl.multiple_of(begin + tile * KEY_TILE, HALF)
        for head in range(KEY_VALUE_HEADS):
            value = window[pl.ds(at, KEY_TILE), pl.ds(KEY_WIDTH + head * HEAD_WIDTH, HEAD_WIDTH)]
            peak = peaks[head]
            weights = jnp.exp2(
                (scores[head, tile] - jnp.concatenate([peak, peak], axis=1)) * EXPONENT_SCALE
            )
            added = jnp.dot(
                weights.astype(jnp.bfloat16),
                jnp.concatenate([value, jnp.ones_like(value)], axis=1),
                preferred_element_type=jnp.float32,
            )
            sums[head] = added if first else sums[head] + added

    def loop(body):
        body(0, True)

        def step(tile, _):
            body(tile, False)
            return 0

        lax.fori_loop(1, tiles, step, 0)

    loop(tile_scores)
    for head in range(KEY_VALUE_HEADS):
        peaks[head] = jnp.broadcast_to(
            jnp.max(peaks[head], axis=1, keepdims=True), (ROWS, HEAD_WIDTH)
        )
    loop(tile_sums)
    for head in range(KEY_VALUE_HEADS):
        summed = sums[head]
        result = (summed[:, :HEAD_WIDTH] * (1.0 / summed[:, HEAD_WIDTH:])).astype(jnp.bfloat16)
        for k in range(HEADS_PER_KEY):
            out_ref[
                out_slot, :, pl.ds((head * HEADS_PER_KEY + k) * HEAD_WIDTH, HEAD_WIDTH)
            ] = result[k * PIECE : (k + 1) * PIECE]


def attend_kernel(partners, first, meta, groups, slots, lengths, *refs):
    count = len(partners)
    arrived = refs[:count]
    own, left1, left2, far2, right, far3_low, far3_high, back4 = refs[count : count + 8]
    out = refs[count + 8 + (0 if first else 1)]
    listed, query, window, bias, *scratch = refs[-12:-4]
    result, query_sems, window_sems, out_sems = refs[-4:]
    shard = meta[1]
    line_at = lax.rem(shard, LINE)

    total = jnp.int32(0)
    for i, partner in enumerate(partners):
        for here, place, slot in arrivals(meta, groups, slots, partner):

            @pl.when(here)
            def _():
                listed[0, total] = (i * CAPACITY + place) * PIECE
                listed[1, total] = slot

            total = total + here.astype(jnp.int32)

    def query_copy(i):
        rows = CAPACITY * PIECE
        return pltpu.make_async_copy(
            arrived[i], query.at[pl.ds(i * rows, rows)], query_sems.at[i]
        )

    def window_copy(source, block):
        return pltpu.make_async_copy(
            source, window.at[pl.ds(block * BLOCK, BLOCK)], window_sems.at[block]
        )

    def half_copy(source, part):
        return pltpu.make_async_copy(
            source, window.at[pl.ds(BLOCK + part * HALF, HALF)], window_sems.at[1 + part * BACK]
        )

    @pl.when(total > 0)
    def _():
        for i in range(count):
            query_copy(i).start()
        window_copy(own, BACK).start()
        window_copy(back4, 0).start()

        @pl.when(line_at == LINE - 1)
        def _():
            for part in range(2):
                half_copy(right.at[pl.ds(part * HALF, HALF)], part).start()

        @pl.when(line_at < LINE - 1)
        def _():
            half_copy(far3_low, 0).start()
            half_copy(far3_high, 1).start()

        for block, least, near, far in ((3, 1, left1, left2), (2, 2, left2, far2)):

            @pl.when(line_at >= least)
            def _():
                window_copy(near, block).start()

            @pl.when(line_at < least)
            def _():
                window_copy(far, block).start()

        for i in range(count):
            query_copy(i).wait()
        for block in (0, 2, 3, BACK):
            window_copy(own, block).wait()
        for part in range(2):
            half_copy(far3_low, part).wait()

        def out_copy(index, slot):
            at = lax.rem(index, 2)
            return pltpu.make_async_copy(
                result.at[at], out.at[pl.ds(slot * PIECE, PIECE)], out_sems.at[at]
            )

        shape = (ROWS, HEAD_WIDTH)
        chosen = lax.broadcasted_iota(jnp.int32, shape, 0) % PIECE
        chooser = jnp.where(chosen == lax.broadcasted_iota(jnp.int32, shape, 1), 1.0, 0.0)
        for head in range(KEY_VALUE_HEADS):
            scratch[0][head, :, pl.ds(HEAD_WIDTH, HEAD_WIDTH)] = chooser.astype(jnp.bfloat16)

        def one_piece(index, _):
            row = pl.multiple_of(listed[0, index], PIECE)
            slot = listed[1, index]
            base = (shard - BACK) * BLOCK
            begin = shard * BLOCK + slot * PIECE
            place = begin + lax.broadcasted_iota(jnp.int32, (1, HEAD_WIDTH), 1)
            start = jnp.zeros((1, HEAD_WIDTH), jnp.int32)
            first_start = jnp.int32(0)
            end = jnp.int32(0)
            for d in range(NDOC):
                end = end + lengths[0, d]
                start = jnp.where(place >= end, end, start)
                first_start = jnp.where(begin >= end, end, first_start)
            stop = (begin - base + PIECE - 1) // HALF + 1
            tiles = (stop - (first_start - base) // HALF + 1) // 2
            begin_at = jnp.maximum(stop - 2 * tiles, 0) * HALF
            key_at = base + lax.broadcasted_iota(jnp.int32, (KEY_TILE, HEAD_WIDTH), 0)

            def one_bias(k, _):
                tile_at = pl.multiple_of(begin_at + k * KEY_TILE, HALF)
                at = key_at + tile_at
                bias[pl.ds(tile_at, KEY_TILE), :] = jnp.where(
                    (at >= start) & (at <= place), 0.0, MASKED
                ).astype(jnp.bfloat16)
                return 0

            lax.fori_loop(0, tiles, one_bias, 0)

            @pl.when(index >= 2)
            def _():
                out_copy(index, 0).wait()

            piece_attention(
                tiles, row, begin_at, query, window, bias, scratch, result, lax.rem(index, 2)
            )
            out_copy(index, slot).start()
            return 0

        lax.fori_loop(0, total, one_piece, 0)

        @pl.when(total >= 2)
        def _():
            out_copy(total, 0).wait()

        out_copy(total + 1, 0).wait()


def attend(partners, meta, groups, slots, lengths, arrived, blocks, out):
    first = out is None
    count = len(partners)
    operands = [meta, groups, slots, lengths, *arrived, *blocks] + ([] if first else [out])
    return pl.pallas_call(
        functools.partial(attend_kernel, partners, first),
        out_shape=jax.ShapeDtypeStruct((BLOCK, QUERY_WIDTH), jnp.bfloat16),
        in_specs=[SMEM] * 4 + [HBM] * (len(operands) - 4),
        out_specs=HBM,
        scratch_shapes=[
            pltpu.SMEM((2, count * CAPACITY), jnp.int32),
            pltpu.VMEM((count * CAPACITY * PIECE, QUERY_WIDTH), jnp.bfloat16),
            pltpu.VMEM(((BACK + 1) * BLOCK, 2 * KEY_WIDTH), jnp.bfloat16),
            pltpu.VMEM(((BACK + 1) * BLOCK, HEAD_WIDTH), jnp.bfloat16),
            pltpu.VMEM((KEY_VALUE_HEADS, ROWS, 2 * HEAD_WIDTH), jnp.bfloat16),
            pltpu.VMEM((KEY_VALUE_HEADS, MOST_TILES, ROWS, KEY_TILE), jnp.float32),
            pltpu.VMEM((KEY_VALUE_HEADS, ROWS, HEAD_WIDTH), jnp.float32),
            pltpu.VMEM((KEY_VALUE_HEADS, ROWS, 2 * HEAD_WIDTH), jnp.float32),
            pltpu.VMEM((2, PIECE, QUERY_WIDTH), jnp.bfloat16),
            pltpu.SemaphoreType.DMA((count,)),
            pltpu.SemaphoreType.DMA((BACK + 2,)),
            pltpu.SemaphoreType.DMA((2,)),
        ],
        input_output_aliases={} if first else {len(operands) - 1: 0},
        compiler_params=pltpu.CompilerParams(vmem_limit_bytes=40 << 20),
        name="attend",
    )(*operands)


def exchange(array, partner):
    if partner == 0:
        return array
    return lax.ppermute(array, "rep", [(g, g ^ partner) for g in range(GROUPS)])


def window_blocks(own, shards):
    line_at = lax.rem(lax.axis_index("sp"), LINE)

    def hop(array, pairs):
        return lax.ppermute(array, "sp", pairs)

    def along(froms, step):
        return [
            (z * LINE + x, z * LINE + (x + step) % LINE)
            for z in range(shards // LINE)
            for x in froms
        ]

    lines = shards // LINE
    half = own.shape[0] // 2
    back4 = hop(own, [(s, s + LINE) for s in range(shards - LINE)])
    right = hop(own, along((0, 1, 2, 3), -1))
    left1 = hop(own, along((0, 1, 2), 1))

    def down(froms, step):
        return [(z * LINE + x, (z + 1) * LINE + x + step) for z in range(lines - 1) for x in froms]

    far2 = hop(right, down((1, 2), -1))
    far3_low = hop(back4[:half], along((1, 2, 3), -1))
    far3_high = hop(right[half:], down((0, 1, 2), 0))
    left2 = hop(jnp.where(line_at == LINE - 1, back4, left1), along((1, 2, 3), 1))
    return own, left1, left2, far2, right, far3_low, far3_high, back4


KEY_ORDER = (2, 6, 3, 7, 4, 5, 1)
QUERY_AFTER = ((1, ()), (2, ()), (6, ()), (3, (1,)), (7, (2,)), (4, (6,)), (5, (3,)))
CHUNKS = ((0, 1, 2, 6), (3, 7), (4,), (5,))


def shards(queries, keys, values, doc_lengths, dest_group, dest_slot):
    meta = jnp.stack([lax.axis_index("rep"), lax.axis_index("sp")]).astype(jnp.int32)
    key_packed = pack(meta, dest_group, keys, values)
    query_packed = list(pack(meta, dest_group, queries))
    key_arrived = {0: key_packed[0]}
    query_arrived = {0: query_packed[0]}
    for partner in KEY_ORDER:
        key_arrived[partner] = exchange(key_packed[partner], partner)
    arrived_keys = [key_arrived[partner] for partner in KEY_ORDER]
    for partner, after in QUERY_AFTER:
        before = [query_arrived[earlier] for earlier in after] or arrived_keys
        array, _ = lax.optimization_barrier((query_packed[partner], before))
        query_arrived[partner] = exchange(array, partner)
    key_arrived[1], query_packed[0] = lax.optimization_barrier((key_arrived[1], query_packed[0]))
    query_arrived[0] = query_packed[0]
    own = place_keys(meta, dest_group, dest_slot, [key_arrived[r] for r in range(GROUPS)])
    own, query_arrived[1] = lax.optimization_barrier((own, query_arrived[1]))
    blocks = window_blocks(own, lax.axis_size("sp"))
    out = None
    for partners in CHUNKS:
        out = attend(
            partners,
            meta,
            dest_group,
            dest_slot,
            doc_lengths,
            [query_arrived[r] for r in partners],
            blocks,
            out,
        )
    return out


def solution(mesh):
    return jax.shard_map(
        shards,
        mesh=mesh,
        in_specs=(
            P(("rep", "sp"), None),
            P(("rep", "sp"), None),
            P(("rep", "sp"), None),
            P("rep", None),
            P(),
            P(),
        ),
        out_specs=P(("rep", "sp"), None),
        check_vma=False,
    )
```

```python
import functools
import math

import jax
import jax.numpy as jnp
from jax import lax
from jax.experimental import pallas as pl
from jax.experimental.pallas import tpu as pltpu
from jax.sharding import PartitionSpec as P

QUERY_HEADS = 64
KEY_VALUE_HEADS = 8
HEADS_PER_KEY = QUERY_HEADS // KEY_VALUE_HEADS
HEAD_WIDTH = 128
PIECES = 8
PIECE = 32
GROUPS = 8
CAPACITY = 2
NDOC = 16
BLOCK = PIECES * PIECE
HALF = BLOCK // 2
ROWS = HEADS_PER_KEY * PIECE
BACK = 4
LINE = 4
KEY_TILE = 256
MOST_TILES = 5
QUERY_WIDTH = QUERY_HEADS * HEAD_WIDTH
KEY_WIDTH = KEY_VALUE_HEADS * HEAD_WIDTH
MASKED = -1e30
EXPONENT_SCALE = 1.0 / math.sqrt(HEAD_WIDTH) / math.log(2.0)

HBM = pl.BlockSpec(memory_space=pltpu.HBM)
VMEM = pl.BlockSpec(memory_space=pltpu.VMEM)
SMEM = pl.BlockSpec(memory_space=pltpu.SMEM)


def pack_kernel(source_count, meta, groups, *refs):
    sources = refs[:source_count]
    outs = refs[source_count : source_count + GROUPS]
    sems = refs[-1]
    group_self, shard = meta[0], meta[1]
    targets = [groups[group_self, shard * PIECES + j] for j in range(PIECES)]

    def copies(j, partner, place):
        column = 0
        made = []
        for k, source in enumerate(sources):
            width = source.shape[1]
            made.append(
                pltpu.make_async_copy(
                    source.at[pl.ds(j * PIECE, PIECE)],
                    outs[partner].at[pl.ds(place * PIECE, PIECE), pl.ds(column, width)],
                    sems.at[k, j],
                )
            )
            column += width
        return made

    for j in range(PIECES):
        place = jnp.int32(0)
        for earlier in range(j):
            place += (targets[earlier] == targets[j]).astype(jnp.int32)
        partner_of = lax.bitwise_xor(targets[j], group_self)
        for partner in range(GROUPS):

            @pl.when(partner_of == partner)
            def _():
                for copy in copies(j, partner, place):
                    copy.start()

    for j in range(PIECES):
        for copy in copies(j, 0, 0):
            copy.wait()


def pack(meta, groups, *sources):
    width = sum(source.shape[1] for source in sources)
    return pl.pallas_call(
        functools.partial(pack_kernel, len(sources)),
        out_shape=[
            jax.ShapeDtypeStruct((CAPACITY * PIECE, width), jnp.bfloat16) for _ in range(GROUPS)
        ],
        in_specs=[SMEM, SMEM] + [VMEM] * len(sources),
        out_specs=[HBM] * GROUPS,
        scratch_shapes=[pltpu.SemaphoreType.DMA((len(sources), PIECES))],
        compiler_params=pltpu.CompilerParams(vmem_limit_bytes=12 << 20),
        name="pack",
    )(meta, groups, *sources)


def arrivals(meta, groups, slots, partner):
    group_self, shard = meta[0], meta[1]
    source = lax.bitwise_xor(group_self, partner)
    found = []
    place = jnp.int32(0)
    for j in range(PIECES):
        here = groups[source, shard * PIECES + j] == group_self
        found.append((here, place, slots[source, shard * PIECES + j]))
        place += here.astype(jnp.int32)
    return found


def place_kernel(meta, groups, slots, *refs):
    arrived, out, sems = refs[:GROUPS], refs[GROUPS], refs[GROUPS + 1]

    def copy_of(partner, place, slot):
        return pltpu.make_async_copy(
            arrived[partner].at[pl.ds(place * PIECE, PIECE)],
            out.at[pl.ds(slot * PIECE, PIECE)],
            sems.at[slot],
        )

    for partner in range(GROUPS):
        for here, place, slot in arrivals(meta, groups, slots, partner):

            @pl.when(here)
            def _():
                copy_of(partner, place, slot).start()

    for slot in range(PIECES):
        copy_of(0, 0, slot).wait()


def place_keys(meta, groups, slots, arrived):
    return pl.pallas_call(
        place_kernel,
        out_shape=jax.ShapeDtypeStruct((BLOCK, arrived[0].shape[1]), jnp.bfloat16),
        in_specs=[SMEM] * 3 + [VMEM] * GROUPS,
        out_specs=HBM,
        scratch_shapes=[pltpu.SemaphoreType.DMA((PIECES,))],
        compiler_params=pltpu.CompilerParams(vmem_limit_bytes=4 << 20),
        name="place_keys",
    )(meta, groups, slots, *arrived)


def piece_attention(tiles, row, begin, query_ref, window, bias, scratch, out_ref, out_slot):
    rows, scores, peaks, sums = scratch
    for head in range(KEY_VALUE_HEADS):
        for k in range(HEADS_PER_KEY):
            rows[head, pl.ds(k * PIECE, PIECE), pl.ds(0, HEAD_WIDTH)] = query_ref[
                pl.ds(row, PIECE), pl.ds((head * HEADS_PER_KEY + k) * HEAD_WIDTH, HEAD_WIDTH)
            ]

    def tile_scores(tile, first):
        at = pl.multiple_of(begin + tile * KEY_TILE, HALF)
        masks = bias[pl.ds(at, KEY_TILE), :]
        for head in range(KEY_VALUE_HEADS):
            key = window[pl.ds(at, KEY_TILE), pl.ds(head * HEAD_WIDTH, HEAD_WIDTH)]
            score = lax.dot_general(
                rows[head],
                jnp.concatenate([key, masks], axis=1),
                (((1,), (1,)), ((), ())),
                preferred_element_type=jnp.float32,
            )
            scores[head, tile] = score
            peak = jnp.maximum(score[:, :HEAD_WIDTH], score[:, HEAD_WIDTH:])
            peaks[head] = peak if first else jnp.maximum(peaks[head], peak)

    def tile_sums(tile, first):
        at = pl.multiple_of(begin + tile * KEY_TILE, HALF)
        for head in range(KEY_VALUE_HEADS):
            value = window[pl.ds(at, KEY_TILE), pl.ds(KEY_WIDTH + head * HEAD_WIDTH, HEAD_WIDTH)]
            peak = peaks[head]
            weights = jnp.exp2(
                (scores[head, tile] - jnp.concatenate([peak, peak], axis=1)) * EXPONENT_SCALE
            )
            added = jnp.dot(
                weights.astype(jnp.bfloat16),
                jnp.concatenate([value, jnp.ones_like(value)], axis=1),
                preferred_element_type=jnp.float32,
            )
            sums[head] = added if first else sums[head] + added

    def loop(body):
        body(0, True)

        def step(tile, _):
            body(tile, False)
            return 0

        lax.fori_loop(1, tiles, step, 0)

    loop(tile_scores)
    for head in range(KEY_VALUE_HEADS):
        peaks[head] = jnp.broadcast_to(
            jnp.max(peaks[head], axis=1, keepdims=True), (ROWS, HEAD_WIDTH)
        )
    loop(tile_sums)
    for head in range(KEY_VALUE_HEADS):
        summed = sums[head]
        result = (summed[:, :HEAD_WIDTH] * (1.0 / summed[:, HEAD_WIDTH:])).astype(jnp.bfloat16)
        for k in range(HEADS_PER_KEY):
            out_ref[
                out_slot, :, pl.ds((head * HEADS_PER_KEY + k) * HEAD_WIDTH, HEAD_WIDTH)
            ] = result[k * PIECE : (k + 1) * PIECE]


def attend_kernel(partners, first, meta, groups, slots, lengths, *refs):
    count = len(partners)
    arrived = refs[:count]
    own, left1, left2, far2, right, far3_low, far3_high, back4 = refs[count : count + 8]
    out = refs[count + 8 + (0 if first else 1)]
    listed, query, window, bias, *scratch = refs[-12:-4]
    result, query_sems, window_sems, out_sems = refs[-4:]
    shard = meta[1]
    line_at = lax.rem(shard, LINE)

    total = jnp.int32(0)
    for i, partner in enumerate(partners):
        for here, place, slot in arrivals(meta, groups, slots, partner):

            @pl.when(here)
            def _():
                listed[0, total] = (i * CAPACITY + place) * PIECE
                listed[1, total] = slot

            total = total + here.astype(jnp.int32)

    def query_copy(i):
        rows = CAPACITY * PIECE
        return pltpu.make_async_copy(
            arrived[i], query.at[pl.ds(i * rows, rows)], query_sems.at[i]
        )

    def window_copy(source, block):
        return pltpu.make_async_copy(
            source, window.at[pl.ds(block * BLOCK, BLOCK)], window_sems.at[block]
        )

    def half_copy(source, part):
        return pltpu.make_async_copy(
            source, window.at[pl.ds(BLOCK + part * HALF, HALF)], window_sems.at[1 + part * BACK]
        )

    @pl.when(total > 0)
    def _():
        for i in range(count):
            query_copy(i).start()
        window_copy(own, BACK).start()
        window_copy(back4, 0).start()

        @pl.when(line_at == LINE - 1)
        def _():
            for part in range(2):
                half_copy(right.at[pl.ds(part * HALF, HALF)], part).start()

        @pl.when(line_at < LINE - 1)
        def _():
            half_copy(far3_low, 0).start()
            half_copy(far3_high, 1).start()

        for block, least, near, far in ((3, 1, left1, left2), (2, 2, left2, far2)):

            @pl.when(line_at >= least)
            def _():
                window_copy(near, block).start()

            @pl.when(line_at < least)
            def _():
                window_copy(far, block).start()

        for i in range(count):
            query_copy(i).wait()
        for block in (0, 2, 3, BACK):
            window_copy(own, block).wait()
        for part in range(2):
            half_copy(far3_low, part).wait()

        def out_copy(index, slot):
            at = lax.rem(index, 2)
            return pltpu.make_async_copy(
                result.at[at], out.at[pl.ds(slot * PIECE, PIECE)], out_sems.at[at]
            )

        shape = (ROWS, HEAD_WIDTH)
        chosen = lax.broadcasted_iota(jnp.int32, shape, 0) % PIECE
        chooser = jnp.where(chosen == lax.broadcasted_iota(jnp.int32, shape, 1), 1.0, 0.0)
        for head in range(KEY_VALUE_HEADS):
            scratch[0][head, :, pl.ds(HEAD_WIDTH, HEAD_WIDTH)] = chooser.astype(jnp.bfloat16)

        def one_piece(index, _):
            row = pl.multiple_of(listed[0, index], PIECE)
            slot = listed[1, index]
            base = (shard - BACK) * BLOCK
            begin = shard * BLOCK + slot * PIECE
            place = begin + lax.broadcasted_iota(jnp.int32, (1, HEAD_WIDTH), 1)
            start = jnp.zeros((1, HEAD_WIDTH), jnp.int32)
            first_start = jnp.int32(0)
            end = jnp.int32(0)
            for d in range(NDOC):
                end = end + lengths[0, d]
                start = jnp.where(place >= end, end, start)
                first_start = jnp.where(begin >= end, end, first_start)
            stop = (begin - base + PIECE - 1) // HALF + 1
            tiles = (stop - (first_start - base) // HALF + 1) // 2
            begin_at = jnp.maximum(stop - 2 * tiles, 0) * HALF
            key_at = base + lax.broadcasted_iota(jnp.int32, (KEY_TILE, HEAD_WIDTH), 0)

            def one_bias(k, _):
                tile_at = pl.multiple_of(begin_at + k * KEY_TILE, HALF)
                at = key_at + tile_at
                bias[pl.ds(tile_at, KEY_TILE), :] = jnp.where(
                    (at >= start) & (at <= place), 0.0, MASKED
                ).astype(jnp.bfloat16)
                return 0

            lax.fori_loop(0, tiles, one_bias, 0)

            @pl.when(index >= 2)
            def _():
                out_copy(index, 0).wait()

            piece_attention(
                tiles, row, begin_at, query, window, bias, scratch, result, lax.rem(index, 2)
            )
            out_copy(index, slot).start()
            return 0

        lax.fori_loop(0, total, one_piece, 0)

        @pl.when(total >= 2)
        def _():
            out_copy(total, 0).wait()

        out_copy(total + 1, 0).wait()


def attend(partners, meta, groups, slots, lengths, arrived, blocks, out):
    first = out is None
    count = len(partners)
    operands = [meta, groups, slots, lengths, *arrived, *blocks] + ([] if first else [out])
    return pl.pallas_call(
        functools.partial(attend_kernel, partners, first),
        out_shape=jax.ShapeDtypeStruct((BLOCK, QUERY_WIDTH), jnp.bfloat16),
        in_specs=[SMEM] * 4 + [HBM] * (len(operands) - 4),
        out_specs=HBM,
        scratch_shapes=[
            pltpu.SMEM((2, count * CAPACITY), jnp.int32),
            pltpu.VMEM((count * CAPACITY * PIECE, QUERY_WIDTH), jnp.bfloat16),
            pltpu.VMEM(((BACK + 1) * BLOCK, 2 * KEY_WIDTH), jnp.bfloat16),
            pltpu.VMEM(((BACK + 1) * BLOCK, HEAD_WIDTH), jnp.bfloat16),
            pltpu.VMEM((KEY_VALUE_HEADS, ROWS, 2 * HEAD_WIDTH), jnp.bfloat16),
            pltpu.VMEM((KEY_VALUE_HEADS, MOST_TILES, ROWS, KEY_TILE), jnp.float32),
            pltpu.VMEM((KEY_VALUE_HEADS, ROWS, HEAD_WIDTH), jnp.float32),
            pltpu.VMEM((KEY_VALUE_HEADS, ROWS, 2 * HEAD_WIDTH), jnp.float32),
            pltpu.VMEM((2, PIECE, QUERY_WIDTH), jnp.bfloat16),
            pltpu.SemaphoreType.DMA((count,)),
            pltpu.SemaphoreType.DMA((BACK + 2,)),
            pltpu.SemaphoreType.DMA((2,)),
        ],
        input_output_aliases={} if first else {len(operands) - 1: 0},
        compiler_params=pltpu.CompilerParams(vmem_limit_bytes=40 << 20),
        name="attend",
    )(*operands)


def exchange(array, partner):
    if partner == 0:
        return array
    return lax.ppermute(array, "rep", [(g, g ^ partner) for g in range(GROUPS)])


def window_blocks(own, shards):
    line_at = lax.rem(lax.axis_index("sp"), LINE)

    def hop(array, pairs):
        return lax.ppermute(array, "sp", pairs)

    def along(froms, step):
        return [
            (z * LINE + x, z * LINE + (x + step) % LINE)
            for z in range(shards // LINE)
            for x in froms
        ]

    lines = shards // LINE
    half = own.shape[0] // 2
    back4 = hop(own, [(s, s + LINE) for s in range(shards - LINE)])
    right = hop(own, along((0, 1, 2, 3), -1))
    left1 = hop(own, along((0, 1, 2), 1))

    def down(froms, step):
        return [(z * LINE + x, (z + 1) * LINE + x + step) for z in range(lines - 1) for x in froms]

    far2 = hop(right, down((1, 2), -1))
    far3_low = hop(back4[:half], along((1, 2, 3), -1))
    far3_high = hop(right[half:], down((0, 1, 2), 0))
    left2 = hop(jnp.where(line_at == LINE - 1, back4, left1), along((1, 2, 3), 1))
    return own, left1, left2, far2, right, far3_low, far3_high, back4


KEY_ORDER = (2, 6, 3, 7, 4, 5, 1)
QUERY_AFTER = ((1, ()), (2, ()), (6, ()), (3, (1,)), (7, (2,)), (4, (6,)), (5, (3,)))
CHUNKS = ((0, 1, 2, 6), (3, 7), (4,), (5,))


def shards(queries, keys, values, doc_lengths, dest_group, dest_slot):
    meta = jnp.stack([lax.axis_index("rep"), lax.axis_index("sp")]).astype(jnp.int32)
    key_packed = pack(meta, dest_group, keys, values)
    query_packed = list(pack(meta, dest_group, queries))
    key_arrived = {0: key_packed[0]}
    query_arrived = {0: query_packed[0]}
    for partner in KEY_ORDER:
        key_arrived[partner] = exchange(key_packed[partner], partner)
    arrived_keys = [key_arrived[partner] for partner in KEY_ORDER]
    for partner, after in QUERY_AFTER:
        before = [query_arrived[earlier] for earlier in after] or arrived_keys
        array, _ = lax.optimization_barrier((query_packed[partner], before))
        query_arrived[partner] = exchange(array, partner)
    key_arrived[1], query_packed[0] = lax.optimization_barrier((key_arrived[1], query_packed[0]))
    query_arrived[0] = query_packed[0]
    own = place_keys(meta, dest_group, dest_slot, [key_arrived[r] for r in range(GROUPS)])
    own, query_arrived[1] = lax.optimization_barrier((own, query_arrived[1]))
    blocks = window_blocks(own, lax.axis_size("sp"))
    out = None
    for partners in CHUNKS:
        out = attend(
            partners,
            meta,
            dest_group,
            dest_slot,
            doc_lengths,
            [query_arrived[r] for r in partners],
            blocks,
            out,
        )
    return out


def solution(mesh):
    return jax.shard_map(
        shards,
        mesh=mesh,
        in_specs=(
            P(("rep", "sp"), None),
            P(("rep", "sp"), None),
            P(("rep", "sp"), None),
            P("rep", None),
            P(),
            P(),
        ),
        out_specs=P(("rep", "sp"), None),
        check_vma=False,
    )
```
